512 devices in a mesh: space: 16 (over x, y_lo, core), term: 32 (over z, y_hi).
Axes of the slice: x: 4, y: 8 (y_hi: 4, y_lo: 2; y = y_hi * 2 + y_lo), z: 8, core: 2. Of those that a mesh axis runs over, the one named last changes fastest.
Arguments:
- right_modes: float32 [512, 64, 256], P(('space', 'term')), may hold values from -0.015625 to 0.015625
- adjoint_modes: float32 [512, 64, 256], P(('space', 'term')), may hold values from -6 to 6
- conductivity_terms: float32 [512, 256, 256], P('space', 'term'), may hold values from -6 to 6
Outputs:
- reduced_blocks: float32 [256, 4096], P('term', 'space')
The draws below stay inside these ranges and needn't reach their ends.
All inputs are finite; a program needn't handle non-finite values.
Results may differ from the reference program's by a relative error of at most 0.000098.
Values sent between devices are 32-bit elements; how exact they have to be, the bound alone decides.
A program may use at most 64 MiB of HBM per device.

```python
import jax
import jax.numpy as jnp
from jax import lax

R = 64
Q = 256
GX = 8
GY = 32
NZ = 512
PLANE = 256


def steps_of(rng, extent, pieces, low, high):
    factor_of = 1.0
    for axis_at, blocks in pieces:
        heights = jax.random.uniform(jax.random.fold_in(jax.random.fold_in(rng, 6), axis_at), (blocks,), jnp.float32, low / len(pieces), high / len(pieces))
        factor_of = factor_of * jnp.repeat(jnp.exp(heights), extent[axis_at] // blocks).reshape((-1,) + (1,) * (len(extent) - 1 - axis_at))
    return factor_of


def noise(own_key, extent, scale, most, pieces=(), dtype=jnp.bfloat16):
    entries = scale * jax.random.normal(own_key, extent, jnp.float32)
    if pieces:
        entries = entries * steps_of(own_key, extent, pieces, -0.22, 0.18)
    return jnp.clip(entries, -most, most).astype(dtype)


def setup_inputs(seed: int = 0) -> dict:
    key_of = jax.random.split(jax.random.key(seed), 4)
    return {
        "right_modes": noise(key_of[0], (NZ, R, PLANE), (NZ * GX * GY) ** -0.5, 0.015625, ((0, 512),), jnp.float32),
        "adjoint_modes": noise(key_of[1], (NZ, R, PLANE), 1.0, 6.0, ((0, 512),), jnp.float32),
        "conductivity_terms": noise(key_of[2], (NZ, Q, PLANE), 1.0, 6.0, ((0, 16), (1, 32)), jnp.float32),
    }


def shifted_cells(values, offset):
    zeros = jnp.zeros(values.shape[:-1] + (abs(offset),), jnp.float32)
    if offset > 0:
        return jnp.concatenate([values[..., offset:], zeros], axis=-1)
    return jnp.concatenate([zeros, values[..., :offset]], axis=-1)


def apply_terms(field_pad, coeff_pad, row_len):
    width = field_pad.shape[-1]
    column = jnp.arange(width) % row_len
    keep_next = (column != row_len - 1).astype(jnp.float32)
    keep_prev = (column != 0).astype(jnp.float32)
    centre = field_pad[None, 1:-1]
    coeff = coeff_pad[:, 1:-1, None, :]
    pairs = [
        (field_pad[None, 2:], coeff_pad[:, 2:, None, :]),
        (field_pad[None, :-2], coeff_pad[:, :-2, None, :]),
        (shifted_cells(centre, row_len), shifted_cells(coeff, row_len)),
        (shifted_cells(centre, -row_len), shifted_cells(coeff, -row_len)),
        (shifted_cells(centre, 1) * keep_next, shifted_cells(coeff, 1) * keep_next),
        (shifted_cells(centre, -1) * keep_prev, shifted_cells(coeff, -1) * keep_prev),
    ]
    result = jnp.zeros(coeff.shape[:2] + centre.shape[2:], jnp.float32)
    for other_field, other_coeff in pairs:
        result = result + 0.5 * (coeff + other_coeff) * (centre - other_field)
    return result


def project(adjoint, image):
    return jnp.einsum("zrp,gzsp->grs", adjoint, image, precision=lax.Precision.HIGHEST)


def reference(right_modes, adjoint_modes, conductivity_terms):
    field_pad = jnp.pad(right_modes, ((1, 1), (0, 0), (0, 0)))
    coeff_pad = jnp.moveaxis(jnp.pad(conductivity_terms, ((1, 1), (0, 0), (0, 0))), 1, 0)

    def one_term(coeff):
        image = apply_terms(field_pad, coeff[None], GY)
        return project(adjoint_modes, image)[0]

    blocks = lax.map(one_term, coeff_pad)
    return blocks.reshape(Q, R * R)
```

```python
import jax
import jax.numpy as jnp
from jax import lax
from jax.experimental import pallas as pl
from jax.experimental.pallas import tpu as pltpu
from jax.sharding import PartitionSpec as P

MESH = pl.DeviceIdType.MESH
GY = 32
NX, NL, NC = 4, 2, 2
NZ, NH = 8, 4
VMEM = pl.BlockSpec(memory_space=pltpu.VMEM)


def remote(src, dst, send, recv, space, term):
    return pltpu.make_async_remote_copy(
        src_ref=src, dst_ref=dst, send_sem=send, recv_sem=recv,
        device_id=(space, term), device_id_type=MESH,
    )


def gather_kernel(right_ref, adjoint_ref, coeff_ref, field_ref, terms_ref, send_sem, recv_sem, term_send, term_recv):
    spaces, terms = NX * NL * NC, NZ * NH
    space, term = lax.axis_index("space"), lax.axis_index("term")
    z, h = lax.div(term, NH), lax.rem(term, NH)
    after = z * NH + lax.rem(h + 1, NH)
    before = z * NH + lax.rem(h + NH - 1, NH)
    up = (lax.rem(space + jnp.where(z == NZ - 1, 1, 0), spaces), lax.rem(term + NH, terms))
    down = (lax.rem(space + jnp.where(z == 0, spaces - 1, 0), spaces), lax.rem(term + terms - NH, terms))
    column = [lax.rem(z + step, NZ) for step in range(1, NZ)]

    barrier = pltpu.get_barrier_semaphore()
    partners = [(space, after), (space, before), up, down] + [(space, other * NH + h) for other in column]
    for partner in partners:
        pl.semaphore_signal(barrier, inc=1, device_id=partner, device_id_type=MESH)
    pl.semaphore_wait(barrier, len(partners))

    own = h + 1
    sources = (adjoint_ref.at[0], right_ref.at[0])

    def field(slot, kind, source, number, target):
        return remote(source, field_ref.at[slot, kind], send_sem.at[number], recv_sem.at[slot, kind], *target)

    def held(slot, kind, number, target):
        return field(slot, kind, field_ref.at[slot, kind], number, target)

    def arrival(slot, kind):
        pltpu.make_async_copy(field_ref.at[slot, kind], field_ref.at[slot, kind], recv_sem.at[slot, kind]).wait()

    first = []
    for kind in (0, 1):
        first.append(field(own, kind, sources[kind], kind, (space, after)))
        first.append(field(own, kind, sources[kind], 2 + kind, (space, before)))
    to_up = [field(0, kind, sources[kind], 4 + kind, up) for kind in (0, 1)]
    to_down = [field(NH + 1, kind, sources[kind], 4 + kind, down) for kind in (0, 1)]

    @pl.when(h == NH - 1)
    def _():
        for copy in to_up:
            copy.start()

    @pl.when(h == 0)
    def _():
        for copy in to_down:
            copy.start()

    for copy in first:
        copy.start()
    coeff = []
    for step, other in enumerate(column):
        coeff.append(remote(
            coeff_ref.at[pl.ds(other * NH, NH)], terms_ref.at[z], term_send.at[step], term_recv.at[step],
            space, other * NH + h,
        ))
        coeff[-1].start()
    for kind in (0, 1):
        field_ref[own, kind] = sources[kind][...]
    terms_ref[z] = coeff_ref[pl.ds(z * NH, NH)]

    side = ((0, NH - 1, 0, 2), (NH + 1, 0, 2, 0))
    slot_before, slot_after = lax.rem(h + NH - 1, NH) + 1, lax.rem(h + 1, NH) + 1
    opposite = lax.rem(h + 2, NH) + 1

    low = [held(0, kind, 8 + kind, (space, after)) for kind in (0, 1)]
    low += [held(0, kind, 10 + kind, (space, before)) for kind in (0, 1)]
    high = [held(NH + 1, kind, 8 + kind, (space, after)) for kind in (0, 1)]
    high += [held(NH + 1, kind, 10 + kind, (space, before)) for kind in (0, 1)]

    @pl.when(h == NH - 1)
    def _():
        for kind in (0, 1):
            arrival(0, kind)
        for copy in low:
            copy.start()

    @pl.when(h == 0)
    def _():
        for kind in (0, 1):
            arrival(NH + 1, kind)
        for copy in high:
            copy.start()

    arrival(slot_before, 0)
    on_after = held(slot_before, 0, 6, (space, after))
    on_after.start()
    arrival(slot_after, 1)
    on_before = held(slot_after, 1, 7, (space, before))
    on_before.start()

    last = {
        0: [held(0, 1, 12, (space, after))],
        1: [held(NH + 1, 0, 12, (space, after))],
        2: [held(0, 0, 12, (space, before))],
        3: [held(NH + 1, 1, 12, (space, before))],
    }
    entered = {0: NH + 1, 3: 0}
    for which in range(NH):
        @pl.when(h == which)
        def _(which=which):
            for copy in last[which]:
                slot, kind = {0: (0, 1), 1: (NH + 1, 0), 2: (0, 0), 3: (NH + 1, 1)}[which]
                arrival(slot, kind)
                copy.start()
            done = {{0: (0, 1), 1: (NH + 1, 0), 2: (0, 0), 3: (NH + 1, 1)}[which]}
            if which in entered:
                done |= {(entered[which], 0), (entered[which], 1)}
            for slot in (0, NH + 1):
                for kind in (0, 1):
                    if (slot, kind) not in done:
                        arrival(slot, kind)
            for copy in last[which]:
                copy.wait_send()

    arrival(slot_before, 1)
    arrival(slot_after, 0)
    for kind in (0, 1):
        arrival(opposite, kind)
    for copy in coeff:
        copy.wait()
    for copy in first + [on_after, on_before]:
        copy.wait_send()

    @pl.when(h == NH - 1)
    def _():
        for copy in to_up + low:
            copy.wait_send()

    @pl.when(h == 0)
    def _():
        for copy in to_down + high:
            copy.wait_send()


def moved(values, shift, keep):
    return jnp.where(keep, pltpu.roll(values, shift % values.shape[-1], values.ndim - 1), 0.0)


def multiply_kernel(field_ref, terms_ref, out_ref, diff, weights):
    space, term = lax.axis_index("space"), lax.axis_index("term")
    z = lax.div(term, NH)
    lowest = jnp.logical_and(space == 0, z == 0)
    highest = jnp.logical_and(space == NX * NL * NC - 1, z == NZ - 1)
    modes, plane = field_ref.shape[2:]
    cell = lax.broadcasted_iota(jnp.int32, (modes, plane), 1)
    column = lax.rem(cell, GY)
    keeps = ((GY, cell >= GY), (-GY, cell < plane - GY), (1, column != 0), (-1, column != GY - 1))
    for kind in (0, 1):
        for slot in range(NH + 1):
            below, above = field_ref[slot, kind], field_ref[slot + 1, kind]
            if slot == 0:
                below = jnp.where(lowest, 0.0, below)
            if slot == NH:
                above = jnp.where(highest, 0.0, above)
            diff[kind, slot] = above - below
        for slot in range(NH):
            own = field_ref[slot + 1, kind]
            for which, (shift, keep) in enumerate(keeps):
                diff[kind, NH + 1 + NH * which + slot] = own - moved(own, shift, keep)
    for slot in range(NH):
        value = 0.5 * terms_ref[:, slot].reshape(modes, plane)
        high = value.astype(jnp.bfloat16)
        rest = (value - high.astype(jnp.float32)).astype(jnp.bfloat16)
        weights[:, slot * plane:(slot + 1) * plane] = jnp.concatenate([high, rest], axis=0)

    lanes = lax.broadcasted_iota(jnp.int32, (modes, 2 * modes), 1)

    def product(row, index):
        return diff[0, index, pl.ds(row, 1), :] * diff[1, index]

    def step(turn, carry):
        d, j0 = lax.div(turn, 2), lax.rem(turn, 2)
        folded = []
        for j1 in (0, 1):
            row = 4 * d + 2 * j1 + j0
            total = None
            edge = product(row, 0)
            for slot in range(NH):
                upper = product(row, slot + 1)
                value = edge + upper
                edge = upper
                for which in range(4):
                    value = value + product(row, NH + 1 + NH * which + slot)
                high = value.astype(jnp.bfloat16)
                rest = (value - high.astype(jnp.float32)).astype(jnp.bfloat16)
                part = lax.dot_general(
                    jnp.concatenate([high, rest], axis=0), weights[:, slot * plane:(slot + 1) * plane],
                    (((1,), (1,)), ((), ())), preferred_element_type=jnp.float32,
                )
                total = part if total is None else total + part
            total = total[:modes] + total[modes:]
            folded.append(total + pltpu.roll(total, modes, 1))
        out_ref[d, pl.ds(pl.multiple_of(j0 * modes, modes), modes), :] = jnp.where(lanes < modes, folded[0], folded[1])
        return carry

    lax.fori_loop(0, out_ref.shape[0] * 2, step, 0)


def reduce_kernel(part_ref, out_ref, pair_in, mine, slab_in, turned, column_in, pair_sem, slab_sem, column_sem):
    space, term = lax.axis_index("space"), lax.axis_index("term")
    c = lax.rem(space, NC)
    x, l = lax.div(space, NL * NC), lax.rem(lax.div(space, NC), NL)
    z, h = lax.div(term, NH), lax.rem(term, NH)
    places = []
    for dx, dl in ((2, 1), (1, 1), (3, 1), (2, 0), (1, 0), (3, 0), (0, 1), (0, 0)):
        places.append(lax.rem(x + dx, NX) * NL + lax.rem(l + dl, NL))
    column = [lax.rem(z + step, NZ) for step in range(1, NZ)]
    other_core = places[-1] * NC + 1 - c

    barrier = pltpu.get_barrier_semaphore()
    partners = [(other_core, term)] + [(place * NC + c, term) for place in places[:-1]]
    partners += [(space, other * NH + h) for other in column]
    for partner in partners:
        pl.semaphore_signal(barrier, inc=1, device_id=partner, device_id_type=MESH)
    pl.semaphore_wait(barrier, len(partners))

    pair = []
    for number, place in enumerate(places):
        pair.append(remote(
            part_ref.at[place * NC + 1 - c], pair_in.at[number], pair_sem.at[0, number], pair_sem.at[1, number],
            other_core, term,
        ))
        pair[-1].start()
    slab = []
    for number, place in enumerate(places):
        pair[number].wait_recv()
        mine[number] = part_ref[place * NC + c] + pair_in[number]
        if number < len(places) - 1:
            slab.append(remote(
                mine.at[number], slab_in.at[number], slab_sem.at[0, number], slab_sem.at[1, number],
                place * NC + c, term,
            ))
            slab[-1].start()
    total = mine[len(places) - 1]
    for number, copy in enumerate(slab):
        copy.wait_recv()
        total = total + slab_in[number]
    total = total.T
    turned[...] = total.reshape(turned.shape)
    sent = []
    for step, other in enumerate(column):
        sent.append(remote(
            turned.at[:, other], column_in.at[step], column_sem.at[0, step], column_sem.at[1, step],
            space, other * NH + h,
        ))
        sent[-1].start()
    result = turned[:, z]
    for step, copy in enumerate(sent):
        copy.wait_recv()
        result = result + column_in[step]
    width = result.shape[-1]
    out_ref[:, :width] = result[0]
    out_ref[:, width:] = result[1]
    for copy in pair + slab + sent:
        copy.wait_send()


def local(right_modes, adjoint_modes, conductivity_terms):
    modes, plane = right_modes.shape[1:]
    per = conductivity_terms.shape[1]
    spaces = NX * NL * NC
    field, terms = pl.pallas_call(
        gather_kernel,
        out_shape=(
            jax.ShapeDtypeStruct((NH + 2, 2, modes, plane), jnp.float32),
            jax.ShapeDtypeStruct((NZ, NH, per, plane), jnp.float32),
        ),
        in_specs=[VMEM] * 3,
        out_specs=(VMEM, VMEM),
        scratch_shapes=[
            pltpu.SemaphoreType.DMA((13,)),
            pltpu.SemaphoreType.DMA((NH + 2, 2)),
            pltpu.SemaphoreType.DMA((NZ - 1,)),
            pltpu.SemaphoreType.DMA((NZ - 1,)),
        ],
        compiler_params=pltpu.CompilerParams(collective_id=0, has_side_effects=True),
        name="gather_planes",
    )(right_modes, adjoint_modes, conductivity_terms)
    part = pl.pallas_call(
        multiply_kernel,
        out_shape=jax.ShapeDtypeStruct((spaces, 2 * modes, 2 * modes), jnp.float32),
        in_specs=[VMEM] * 2,
        out_specs=VMEM,
        scratch_shapes=[
            pltpu.VMEM((2, 5 * NH + 1, modes, plane), jnp.float32),
            pltpu.VMEM((2 * modes, NH * plane), jnp.bfloat16),
        ],
        name="multiply_planes",
    )(field, terms)
    return pl.pallas_call(
        reduce_kernel,
        out_shape=jax.ShapeDtypeStruct((per, 4 * modes), jnp.float32),
        in_specs=[VMEM],
        out_specs=VMEM,
        scratch_shapes=[
            pltpu.VMEM((NX * NL, 2 * modes, 2 * modes), jnp.float32),
            pltpu.VMEM((NX * NL, 2 * modes, 2 * modes), jnp.float32),
            pltpu.VMEM((NX * NL - 1, 2 * modes, 2 * modes), jnp.float32),
            pltpu.VMEM((2, NZ, per, 2 * modes), jnp.float32),
            pltpu.VMEM((NZ - 1, 2, per, 2 * modes), jnp.float32),
            pltpu.SemaphoreType.DMA((2, NX * NL)),
            pltpu.SemaphoreType.DMA((2, NX * NL - 1)),
            pltpu.SemaphoreType.DMA((2, NZ - 1)),
        ],
        compiler_params=pltpu.CompilerParams(collective_id=1, has_side_effects=True),
        name="reduce_parts",
    )(part)


def solution(mesh):
    placed = (
        P(("space", "term"), None, None),
        P(("space", "term"), None, None),
        P("space", "term", None),
    )
    return jax.shard_map(
        local, mesh=mesh, in_specs=placed, out_specs=P("term", "space"), check_vma=False
    )
```

```python
import jax
import jax.numpy as jnp
from jax import lax
from jax.experimental import pallas as pl
from jax.experimental.pallas import tpu as pltpu
from jax.sharding import PartitionSpec as P

MESH = pl.DeviceIdType.MESH
GY = 32
NX, NL, NC = 4, 2, 2
NZ, NH = 8, 4
VMEM = pl.BlockSpec(memory_space=pltpu.VMEM)


def moved(values, shift, keep):
    return jnp.where(keep, pltpu.roll(values, shift % values.shape[-1], values.ndim - 1), 0.0)


def assemble_kernel(
    right_ref, adjoint_ref, coeff_ref, out_ref,
    field, terms, flat, edges, weights, part, pair_in, mine, slab_in, turned, column_in,
    send_sem, recv_sem, term_sem, pair_sem, slab_sem, column_sem,
):
    spaces, total_terms, places = NX * NL * NC, NZ * NH, NX * NL
    modes, plane = right_ref.shape[1:]
    space, term = lax.axis_index("space"), lax.axis_index("term")
    c = lax.rem(space, NC)
    x, l = lax.div(space, NL * NC), lax.rem(lax.div(space, NC), NL)
    z, h = lax.div(term, NH), lax.rem(term, NH)
    after = (space, z * NH + lax.rem(h + 1, NH))
    before = (space, z * NH + lax.rem(h + NH - 1, NH))
    up = (lax.rem(space + jnp.where(z == NZ - 1, 1, 0), spaces), lax.rem(term + NH, total_terms))
    down = (lax.rem(space + jnp.where(z == 0, spaces - 1, 0), spaces), lax.rem(term + total_terms - NH, total_terms))
    column = [lax.rem(z + step, NZ) for step in range(1, NZ)]

    def place(n):
        return lax.rem(x + lax.rem(n + 1, NX), NX) * NL + lax.rem(l + NL - 1 - lax.div(n, NX), NL)

    def remote(src, dst, send, recv, target):
        return pltpu.make_async_remote_copy(
            src_ref=src, dst_ref=dst, send_sem=send, recv_sem=recv, device_id=target, device_id_type=MESH,
        )

    barrier = pltpu.get_barrier_semaphore()
    partners = [after, before, up, down] + [(space, other * NH + h) for other in column]
    partners += [(place(n) * NC + c, term) for n in range(places - 1)]
    partners += [(place(places - 1) * NC + 1 - c, term)]
    for partner in partners:
        pl.semaphore_signal(barrier, inc=1, device_id=partner, device_id_type=MESH)
    pl.semaphore_wait(barrier, len(partners))

    own, top = h + 1, NH + 1
    slot_before, slot_after = lax.rem(h + NH - 1, NH) + 1, lax.rem(h + 1, NH) + 1
    opposite = lax.rem(h + 2, NH) + 1
    sources = (adjoint_ref.at[0], right_ref.at[0])

    def fresh(slot, kind, number, target):
        return remote(sources[kind], field.at[slot, kind], send_sem.at[number], recv_sem.at[slot, kind], target)

    def held(slot, kind, number, target):
        return remote(
            field.at[slot, kind], field.at[slot, kind], send_sem.at[number], recv_sem.at[slot, kind], target
        )

    def arrival(slot, kind):
        pltpu.make_async_copy(field.at[slot, kind], field.at[slot, kind], recv_sem.at[slot, kind]).wait()

    coeff = []
    for step, other in enumerate(column):
        coeff.append(remote(
            coeff_ref.at[pl.ds(other * NH, NH)], terms.at[z], term_sem.at[0, step], term_sem.at[1, step],
            (space, other * NH + h),
        ))
    first = [fresh(own, 0, 0, after), fresh(own, 1, 1, before), fresh(own, 1, 2, after), fresh(own, 0, 3, before)]
    to_up = [fresh(0, kind, 4 + kind, up) for kind in (0, 1)]
    to_down = [fresh(top, kind, 4 + kind, down) for kind in (0, 1)]
    low = [held(0, 0, 8, after), held(0, 1, 9, before), held(0, 1, 10, after), held(0, 0, 11, before)]
    high = [held(top, 0, 8, after), held(top, 1, 9, before), held(top, 1, 10, after), held(top, 0, 11, before)]
    low_on = [held(0, kind, 8 + kind, before) for kind in (0, 1)]
    high_on = [held(top, kind, 8 + kind, after) for kind in (0, 1)]
    on_after, on_before = held(slot_before, 0, 6, after), held(slot_after, 1, 7, before)

    for copy in first[:2]:
        copy.start()

    @pl.when(h == NH - 1)
    def _():
        for copy in to_up:
            copy.start()

    @pl.when(h == 0)
    def _():
        for copy in to_down:
            copy.start()

    for copy in first[2:] + coeff:
        copy.start()
    terms[z] = coeff_ref[pl.ds(z * NH, NH)]

    cell = lax.broadcasted_iota(jnp.int32, (modes, plane), 1)
    in_row = lax.rem(cell, GY)
    keeps = ((GY, cell >= GY), (-GY, cell < plane - GY), (1, in_row != 0), (-1, in_row != GY - 1))

    def flatten(which, kind, values):
        for number, (shift, keep) in enumerate(keeps):
            flat[kind, 4 * which + number] = values - moved(values, shift, keep)

    for kind in (0, 1):
        values = sources[kind][...]
        field[own, kind] = values
        flatten(0, kind, values)

    @pl.when(h == NH - 1)
    def _():
        for kind in (0, 1):
            arrival(0, kind)
        for copy in low:
            copy.start()

    @pl.when(h == 0)
    def _():
        for kind in (0, 1):
            arrival(top, kind)
        for copy in high:
            copy.start()

    for copy in coeff:
        copy.wait_recv()
    for slot in range(NH):
        value = 0.5 * terms[:, slot].reshape(-1, plane)
        upper = value.astype(jnp.bfloat16)
        lower = (value - upper.astype(jnp.float32)).astype(jnp.bfloat16)
        weights[slot] = jnp.concatenate([upper, lower], axis=0)

    arrival(slot_before, 0)
    on_after.start()
    arrival(slot_after, 1)
    on_before.start()
    arrival(slot_before, 1)
    arrival(slot_after, 0)
    for which, slot in ((1, slot_after), (2, slot_before)):
        for kind in (0, 1):
            flatten(which, kind, field[slot, kind])

    @pl.when(h == 1)
    def _():
        for kind in (0, 1):
            arrival(top, kind)
        for copy in high_on:
            copy.start()

    @pl.when(h == 2)
    def _():
        for kind in (0, 1):
            arrival(0, kind)
        for copy in low_on:
            copy.start()

    lanes = lax.broadcasted_iota(jnp.int32, (modes, 2 * modes), 1)

    def times(value, weight):
        upper = value.astype(jnp.bfloat16)
        lower = (value - upper.astype(jnp.float32)).astype(jnp.bfloat16)
        return lax.dot_general(
            jnp.concatenate([upper, lower], axis=0), weight, (((1,), (1,)), ((), ())),
            preferred_element_type=jnp.float32,
        )

    def level(row, which):
        value = None
        for number in range(4 * which, 4 * which + 4):
            product = flat[0, number, pl.ds(row, 1), :] * flat[1, number]
            value = product if value is None else value + product
        return value

    def folded(totals):
        halves = []
        for total in totals:
            total = total[:modes] + total[modes:]
            halves.append(total + pltpu.roll(total, modes, 1))
        return jnp.where(lanes < modes, *halves)

    def near(turn, carry):
        d, j0 = lax.div(turn, 2), lax.rem(turn, 2)
        totals = []
        for j1 in (0, 1):
            row = 4 * d + 2 * j1 + j0
            total = times(level(row, 0), weights[own - 1])
            total += times(level(row, 1), weights[slot_after - 1])
            total += times(level(row, 2), weights[slot_before - 1])
            totals.append(total)
        part[d, pl.ds(pl.multiple_of(j0 * modes, modes), modes), :] = folded(totals)
        return carry

    lax.fori_loop(0, 2 * spaces, near, 0)

    @pl.when(jnp.logical_or(h == 0, h == NH - 1))
    def _():
        slot = jnp.where(h == 0, 0, top)
        for kind in (0, 1):
            arrival(slot, kind)

    @pl.when(h == 1)
    def _():
        for kind in (0, 1):
            arrival(0, kind)

    @pl.when(h == 2)
    def _():
        for kind in (0, 1):
            arrival(top, kind)

    for kind in (0, 1):
        arrival(opposite, kind)
        flatten(3, kind, field[opposite, kind])

    lowest = jnp.logical_and(space == 0, z == 0)
    highest = jnp.logical_and(space == spaces - 1, z == NZ - 1)
    for kind in (0, 1):
        for slot in range(NH + 1):
            lower, upper = field[slot, kind], field[slot + 1, kind]
            if slot == 0:
                lower = jnp.where(lowest, 0.0, lower)
            if slot == NH:
                upper = jnp.where(highest, 0.0, upper)
            edges[kind, slot] = upper - lower

    def far(d, j0):
        totals = []
        for j1 in (0, 1):
            row = 4 * d + 2 * j1 + j0
            total = times(level(row, 3), weights[opposite - 1])
            lower = edges[0, 0, pl.ds(row, 1), :] * edges[1, 0]
            for slot in range(NH):
                upper = edges[0, slot + 1, pl.ds(row, 1), :] * edges[1, slot + 1]
                total += times(lower + upper, weights[slot])
                lower = upper
            totals.append(total)
        rows = pl.ds(pl.multiple_of(j0 * modes, modes), modes)
        part[d, rows, :] = part[d, rows, :] + folded(totals)

    def pair(n):
        return remote(
            part.at[place(n) * NC + 1 - c], pair_in.at[n], pair_sem.at[0, n], pair_sem.at[1, n],
            (place(places - 1) * NC + 1 - c, term),
        )

    def slab(n):
        return remote(
            mine.at[n], slab_in.at[n], slab_sem.at[0, n], slab_sem.at[1, n], (place(n) * NC + c, term)
        )

    def join(n):
        pair(n).wait_recv()
        mine[n] = part[place(n) * NC + c] + pair_in[n]

    def turn(n, carry):
        def inner(k, carry):
            far(place(n) * NC + lax.rem(c + 1 + lax.div(k, 2), 2), lax.rem(k, 2))
            return carry

        lax.fori_loop(0, 4, inner, 0)
        pair(n).start()

        @pl.when(n > 0)
        def _():
            join(n - 1)
            slab(n - 1).start()

        return carry

    lax.fori_loop(0, places, turn, 0)
    join(places - 1)
    total = mine[places - 1]
    for n in range(places - 1):
        slab(n).wait_recv()
        total = total + slab_in[n]
    total = total.T
    turned[...] = total.reshape(turned.shape)
    sent = []
    for step, other in enumerate(column):
        sent.append(remote(
            turned.at[:, other], column_in.at[step], column_sem.at[0, step], column_sem.at[1, step],
            (space, other * NH + h),
        ))
        sent[-1].start()
    result = turned[:, z]
    for step, copy in enumerate(sent):
        copy.wait_recv()
        result = result + column_in[step]
    width = result.shape[-1]
    out_ref[:, :width] = result[0]
    out_ref[:, width:] = result[1]

    for copy in first + coeff + [on_after, on_before] + sent:
        copy.wait_send()
    for n in range(places):
        pair(n).wait_send()
    for n in range(places - 1):
        slab(n).wait_send()
    for which, copies in enumerate((to_down + high, high_on, low_on, to_up + low)):
        @pl.when(h == which)
        def _(copies=copies):
            for copy in copies:
                copy.wait_send()


def local(right_modes, adjoint_modes, conductivity_terms):
    modes, plane = right_modes.shape[1:]
    per = conductivity_terms.shape[1]
    spaces, places = NX * NL * NC, NX * NL
    block = (2 * modes, 2 * modes)
    return pl.pallas_call(
        assemble_kernel,
        out_shape=jax.ShapeDtypeStruct((per, 4 * modes), jnp.float32),
        in_specs=[VMEM] * 3,
        out_specs=VMEM,
        scratch_shapes=[
            pltpu.VMEM((NH + 2, 2, modes, plane), jnp.float32),
            pltpu.VMEM((NZ, NH, per, plane), jnp.float32),
            pltpu.VMEM((2, 4 * NH, modes, plane), jnp.float32),
            pltpu.VMEM((2, NH + 1, modes, plane), jnp.float32),
            pltpu.VMEM((NH, 2 * NZ * per, plane), jnp.bfloat16),
            pltpu.VMEM((spaces,) + block, jnp.float32),
            pltpu.VMEM((places,) + block, jnp.float32),
            pltpu.VMEM((places,) + block, jnp.float32),
            pltpu.VMEM((max(places - 1, 1),) + block, jnp.float32),
            pltpu.VMEM((2, NZ, per, 2 * modes), jnp.float32),
            pltpu.VMEM((max(NZ - 1, 1), 2, per, 2 * modes), jnp.float32),
            pltpu.SemaphoreType.DMA((12,)),
            pltpu.SemaphoreType.DMA((NH + 2, 2)),
            pltpu.SemaphoreType.DMA((2, max(NZ - 1, 1))),
            pltpu.SemaphoreType.DMA((2, places)),
            pltpu.SemaphoreType.DMA((2, max(places - 1, 1))),
            pltpu.SemaphoreType.DMA((2, max(NZ - 1, 1))),
        ],
        compiler_params=pltpu.CompilerParams(collective_id=0, has_side_effects=True),
        name="assemble_blocks",
    )(right_modes, adjoint_modes, conductivity_terms)


def solution(mesh):
    placed = (
        P(("space", "term"), None, None),
        P(("space", "term"), None, None),
        P("space", "term", None),
    )
    return jax.shard_map(
        local, mesh=mesh, in_specs=placed, out_specs=P("term", "space"), check_vma=False
    )
```

```python
import jax
import jax.numpy as jnp
from jax import lax
from jax.experimental import pallas as pl
from jax.experimental.pallas import tpu as pltpu
from jax.sharding import PartitionSpec as P

MESH = pl.DeviceIdType.MESH
GY = 32
NX, NL, NC = 4, 2, 2
NZ, NH = 8, 4
VMEM = pl.BlockSpec(memory_space=pltpu.VMEM)


def moved(values, shift, keep):
    return jnp.where(keep, pltpu.roll(values, shift % values.shape[-1], values.ndim - 1), 0.0)


def assemble_kernel(
    right_ref, adjoint_ref, coeff_ref, out_ref,
    field, terms, flat, edges, weights, part, pair_in, mine, slab_in, turned, column_in,
    send_sem, recv_sem, term_sem, pair_sem, slab_sem, column_sem,
):
    spaces, total_terms, places = NX * NL * NC, NZ * NH, NX * NL
    modes, plane = right_ref.shape[1:]
    space, term = lax.axis_index("space"), lax.axis_index("term")
    c = lax.rem(space, NC)
    x, l = lax.div(space, NL * NC), lax.rem(lax.div(space, NC), NL)
    z, h = lax.div(term, NH), lax.rem(term, NH)
    odd, mate = lax.rem(h, 2), NH - 1 - h
    index, planes = space * total_terms + term, spaces * total_terms

    def owner(number):
        return lax.div(number, total_terms), lax.rem(number, total_terms)

    above, below = owner(lax.rem(index + 1, planes)), owner(lax.rem(index + planes - 1, planes))
    partner_of_pair = owner(index + 1 - 2 * odd)
    owners = [(step, other) for step in range(NZ) for other in (0, 1)][1:]

    def holder(step, other):
        return lax.rem(z + step, NZ), (mate if other else h)

    def place(n):
        return lax.rem(x + lax.rem(n + 1, NX), NX) * NL + lax.rem(l + NL - 1 - lax.div(n, NX), NL)

    def remote(src, dst, send, recv, target):
        return pltpu.make_async_remote_copy(
            src_ref=src, dst_ref=dst, send_sem=send, recv_sem=recv, device_id=target, device_id_type=MESH,
        )

    barrier = pltpu.get_barrier_semaphore()
    partners = [above, below]
    for step, other in owners:
        far_z, far_h = holder(step, other)
        partners.append((space, far_z * NH + far_h))
    partners += [(place(n) * NC + c, term) for n in range(places - 1)]
    partners += [(place(places - 1) * NC + 1 - c, term)]
    for partner in partners:
        pl.semaphore_signal(barrier, inc=1, device_id=partner, device_id_type=MESH)
    pl.semaphore_wait(barrier, len(partners))

    own = 1 + odd
    sources = (adjoint_ref.at[0], right_ref.at[0])

    def fresh(slot, kind, number, target):
        return remote(sources[kind], field.at[slot, kind], send_sem.at[number], recv_sem.at[slot, kind], target)

    def arrival(slot, kind):
        pltpu.make_async_copy(field.at[slot, kind], field.at[slot, kind], recv_sem.at[slot, kind]).wait()

    first = [fresh(1 - odd, kind, kind, above) for kind in (0, 1)]
    first += [fresh(3 - odd, kind, 2 + kind, below) for kind in (0, 1)]
    relay = [
        remote(
            field.at[3 * odd, kind], field.at[3 * odd, kind], send_sem.at[4 + kind], recv_sem.at[3 * odd, kind],
            partner_of_pair,
        )
        for kind in (0, 1)
    ]
    coeff = []
    for number, (step, other) in enumerate(owners):
        far_z, far_h = holder(step, other)
        coeff.append(remote(
            coeff_ref.at[pl.ds(far_z * NH + 2 * lax.div(far_h, 2), 2)], terms.at[lax.div(h, 2), z],
            term_sem.at[0, number], term_sem.at[1, number], (space, far_z * NH + far_h),
        ))
    @pl.when(odd == 0)
    def _():
        for copy in (first[2], first[3], first[0], first[1]):
            copy.start()

    @pl.when(odd == 1)
    def _():
        for copy in first:
            copy.start()

    for copy in coeff:
        copy.start()
    terms[lax.div(h, 2), z] = coeff_ref[pl.ds(z * NH + 2 * lax.div(h, 2), 2)]

    cell = lax.broadcasted_iota(jnp.int32, (modes, plane), 1)
    in_row = lax.rem(cell, GY)
    keeps = ((GY, cell >= GY), (-GY, cell < plane - GY), (1, in_row != 0), (-1, in_row != GY - 1))

    def flatten(which, kind, values):
        for number, (shift, keep) in enumerate(keeps):
            flat[kind, 4 * which + number] = values - moved(values, shift, keep)

    for kind in (0, 1):
        values = sources[kind][...]
        field[own, kind] = values
        flatten(odd, kind, values)

    outer, inner, last = 3 * odd, 2 - odd, 3 - 3 * odd
    for kind in (0, 1):
        arrival(outer, kind)
        relay[kind].start()
    for copy in coeff:
        copy.wait_recv()
    for slot in (0, 1):
        value = 0.5 * terms[:, :, slot].reshape(-1, plane)
        upper = value.astype(jnp.bfloat16)
        lower = (value - upper.astype(jnp.float32)).astype(jnp.bfloat16)
        weights[:, slot * plane:(slot + 1) * plane] = jnp.concatenate([upper, lower], axis=0)
    for kind in (0, 1):
        arrival(inner, kind)
        flatten(1 - odd, kind, field[inner, kind])
    for kind in (0, 1):
        arrival(last, kind)

    lowest = jnp.logical_and(space == 0, term < 2)
    highest = jnp.logical_and(space == spaces - 1, term >= total_terms - 2)
    for kind in (0, 1):
        values = [field[slot, kind] for slot in range(4)]
        values[0] = jnp.where(lowest, 0.0, values[0])
        values[3] = jnp.where(highest, 0.0, values[3])
        for slot in range(3):
            edges[kind, slot] = values[slot + 1] - values[slot]

    count = weights.shape[0] // 2

    def assemble(d):
        left = []
        for row in range(4):
            row = 4 * d + row
            borders = [edges[0, slot, pl.ds(row, 1), :] * edges[1, slot] for slot in range(3)]
            values = []
            for slot in (0, 1):
                value = borders[slot] + borders[slot + 1]
                for number in range(4 * slot, 4 * slot + 4):
                    value = value + flat[0, number, pl.ds(row, 1), :] * flat[1, number]
                values.append(value)
            value = jnp.concatenate(values, axis=1)
            upper = value.astype(jnp.bfloat16)
            left += [upper, (value - upper.astype(jnp.float32)).astype(jnp.bfloat16)]
        total = lax.dot_general(
            jnp.concatenate(left, axis=0), weights[...], (((1,), (1,)), ((), ())), preferred_element_type=jnp.float32,
        )
        total = total[:, :count] + total[:, count:]
        for row in range(4):
            at = 2 * row * modes
            part[d, row * modes:(row + 1) * modes, :] = total[at:at + modes] + total[at + modes:at + 2 * modes]

    def pair(n):
        return remote(
            part.at[place(n) * NC + 1 - c], pair_in.at[n], pair_sem.at[0, n], pair_sem.at[1, n],
            (place(places - 1) * NC + 1 - c, term),
        )

    def slab(n):
        return remote(
            mine.at[n], slab_in.at[n], slab_sem.at[0, n], slab_sem.at[1, n], (place(n) * NC + c, term)
        )

    def join(n):
        pair(n).wait_recv()
        mine[n] = part[place(n) * NC + c] + pair_in[n]

    def turn(n, carry):
        def step(k, carry):
            assemble(place(n) * NC + lax.rem(c + 1 + k, 2))
            return carry

        lax.fori_loop(0, 2, step, 0)
        pair(n).start()

        @pl.when(n > 0)
        def _():
            join(n - 1)
            slab(n - 1).start()

        return carry

    lax.fori_loop(0, places, turn, 0)
    join(places - 1)
    total = mine[places - 1]
    for n in range(places - 1):
        slab(n).wait_recv()
        total = total + slab_in[n]
    total = total.T
    turned[...] = total.reshape(turned.shape)
    sent = []
    for number, (step, other) in enumerate(owners):
        far_z, far_h = holder(step, other)
        sent.append(remote(
            turned.at[lax.div(far_h, 2), far_z], column_in.at[number], column_sem.at[0, number],
            column_sem.at[1, number], (space, far_z * NH + far_h),
        ))
        sent[-1].start()
    result = turned[lax.div(h, 2), z]
    for number, copy in enumerate(sent):
        copy.wait_recv()
        result = result + column_in[number]
    out_ref[...] = result

    for copy in first + relay + coeff + sent:
        copy.wait_send()
    for n in range(places):
        pair(n).wait_send()
    for n in range(places - 1):
        slab(n).wait_send()


def local(right_modes, adjoint_modes, conductivity_terms):
    modes, plane = right_modes.shape[1:]
    per = conductivity_terms.shape[1]
    spaces, places = NX * NL * NC, NX * NL
    block = (4 * modes, 2 * NZ * per)
    others = 2 * NZ - 1
    return pl.pallas_call(
        assemble_kernel,
        out_shape=jax.ShapeDtypeStruct((per, 4 * modes), jnp.float32),
        in_specs=[VMEM] * 3,
        out_specs=VMEM,
        scratch_shapes=[
            pltpu.VMEM((4, 2, modes, plane), jnp.float32),
            pltpu.VMEM((2, NZ, 2, per, plane), jnp.float32),
            pltpu.VMEM((2, 8, modes, plane), jnp.float32),
            pltpu.VMEM((2, 3, modes, plane), jnp.float32),
            pltpu.VMEM((4 * NZ * per, 2 * plane), jnp.bfloat16),
            pltpu.VMEM((spaces,) + block, jnp.float32),
            pltpu.VMEM((places,) + block, jnp.float32),
            pltpu.VMEM((places,) + block, jnp.float32),
            pltpu.VMEM((max(places - 1, 1),) + block, jnp.float32),
            pltpu.VMEM((2, NZ, per, 4 * modes), jnp.float32),
            pltpu.VMEM((others, per, 4 * modes), jnp.float32),
            pltpu.SemaphoreType.DMA((6,)),
            pltpu.SemaphoreType.DMA((4, 2)),
            pltpu.SemaphoreType.DMA((2, others)),
            pltpu.SemaphoreType.DMA((2, places)),
            pltpu.SemaphoreType.DMA((2, max(places - 1, 1))),
            pltpu.SemaphoreType.DMA((2, others)),
        ],
        compiler_params=pltpu.CompilerParams(collective_id=0, has_side_effects=True),
        name="assemble_blocks",
    )(right_modes, adjoint_modes, conductivity_terms)


def solution(mesh):
    placed = (
        P(("space", "term"), None, None),
        P(("space", "term"), None, None),
        P("space", "term", None),
    )
    return jax.shard_map(
        local, mesh=mesh, in_specs=placed, out_specs=P("term", "space"), check_vma=False
    )
```

```python
import jax
import jax.numpy as jnp
from jax import lax
from jax.experimental import pallas as pl
from jax.experimental.pallas import tpu as pltpu
from jax.sharding import PartitionSpec as P

MESH = pl.DeviceIdType.MESH
GY = 32
NX, NL, NC = 4, 2, 2
NZ, NH = 8, 4
VMEM = pl.BlockSpec(memory_space=pltpu.VMEM)


def moved(values, shift, keep):
    return jnp.where(keep, pltpu.roll(values, shift % values.shape[-1], values.ndim - 1), 0.0)


def assemble_kernel(
    right_ref, adjoint_ref, coeff_ref, out_ref,
    field, terms, flat, edges, weights, part, pair_in, mine, slab_in, near_in, turned, column_in,
    own_sem, send_sem, recv_sem, term_sem, pair_sem, slab_sem, near_sem, column_sem,
):
    spaces, total_terms, places = NX * NL * NC, NZ * NH, NX * NL
    modes, plane = field.shape[2:]
    space, term = lax.axis_index("space"), lax.axis_index("term")
    c = lax.rem(space, NC)
    x, l = lax.div(space, NL * NC), lax.rem(lax.div(space, NC), NL)
    z, h = lax.div(term, NH), lax.rem(term, NH)
    odd, mate = lax.rem(h, 2), NH - 1 - h
    index, planes = space * total_terms + term, spaces * total_terms

    def owner(number):
        return lax.div(number, total_terms), lax.rem(number, total_terms)

    above, below = owner(lax.rem(index + 1, planes)), owner(lax.rem(index + planes - 1, planes))
    partner_of_pair = owner(index + 1 - 2 * odd)
    owners = [(step, other) for step in range(NZ) for other in (0, 1)][1:]

    def holder(step, other):
        return lax.rem(z + step, NZ), (mate if other else h)

    def place(n):
        side = lax.rem(n, 2)
        away = jnp.where(n < 2, 2, jnp.where(n < 6, 1 + 2 * side, 0))
        across = jnp.where(n < 2, side, jnp.where(n < 4, 1 - side, jnp.where(n < 6, side, lax.rem(l + 1 + side, NL))))
        return lax.rem(x + away, NX) * NL + across

    def beside(n):
        return (lax.rem(x + 1 + 2 * lax.rem(n, 2), NX) * NL + l) * NC + c

    def remote(src, dst, send, recv, target):
        return pltpu.make_async_remote_copy(
            src_ref=src, dst_ref=dst, send_sem=send, recv_sem=recv, device_id=target, device_id_type=MESH,
        )

    own = 1 + odd
    sources = (adjoint_ref.at[0], right_ref.at[0])
    brought = [pltpu.make_async_copy(sources[kind], field.at[own, kind], own_sem.at[kind]) for kind in (0, 1)]
    brought.append(pltpu.make_async_copy(
        coeff_ref.at[pl.ds(z * NH + 2 * lax.div(h, 2), 2)], terms.at[lax.div(h, 2), z], own_sem.at[2]
    ))
    for copy in brought:
        copy.start()

    barrier = pltpu.get_barrier_semaphore()
    partners = [above, below]
    for step, other in owners:
        far_z, far_h = holder(step, other)
        partners.append((space, far_z * NH + far_h))
    partners += [(beside(0), term), (beside(1), term), (place(6) * NC + c, term), (place(7) * NC + 1 - c, term)]
    for partner in partners:
        pl.semaphore_signal(barrier, inc=1, device_id=partner, device_id_type=MESH)
    pl.semaphore_wait(barrier, len(partners))

    def fresh(slot, kind, number, target):
        return remote(sources[kind], field.at[slot, kind], send_sem.at[number], recv_sem.at[slot, kind], target)

    def arrival(slot, kind):
        pltpu.make_async_copy(field.at[slot, kind], field.at[slot, kind], recv_sem.at[slot, kind]).wait()

    first = [fresh(1 - odd, kind, kind, above) for kind in (0, 1)]
    first += [fresh(3 - odd, kind, 2 + kind, below) for kind in (0, 1)]
    relay = [
        remote(
            field.at[3 * odd, kind], field.at[3 * odd, kind], send_sem.at[4 + kind], recv_sem.at[3 * odd, kind],
            partner_of_pair,
        )
        for kind in (0, 1)
    ]
    coeff = []
    for number, (step, other) in enumerate(owners):
        far_z, far_h = holder(step, other)
        coeff.append(remote(
            coeff_ref.at[pl.ds(far_z * NH + 2 * lax.div(far_h, 2), 2)], terms.at[lax.div(h, 2), z],
            term_sem.at[0, number], term_sem.at[1, number], (space, far_z * NH + far_h),
        ))
    @pl.when(odd == 0)
    def _():
        for copy in (first[2], first[3], first[0], first[1]):
            copy.start()

    @pl.when(odd == 1)
    def _():
        for copy in first:
            copy.start()

    for copy in coeff:
        copy.start()

    cell = lax.broadcasted_iota(jnp.int32, (modes, plane), 1)
    in_row = lax.rem(cell, GY)
    keeps = ((GY, cell >= GY), (-GY, cell < plane - GY), (1, in_row != 0), (-1, in_row != GY - 1))

    def flatten(which, kind, values):
        for number, (shift, keep) in enumerate(keeps):
            flat[kind, 4 * which + number] = values - moved(values, shift, keep)

    for kind in (0, 1):
        brought[kind].wait()
        flatten(odd, kind, field[own, kind])

    outer, inner, last = 3 * odd, 2 - odd, 3 - 3 * odd
    for kind in (0, 1):
        arrival(outer, kind)
        relay[kind].start()
    brought[2].wait()
    for copy in coeff:
        copy.wait_recv()
    for slot in (0, 1):
        value = 0.5 * terms[:, :, slot].reshape(-1, plane)
        upper = value.astype(jnp.bfloat16)
        lower = (value - upper.astype(jnp.float32)).astype(jnp.bfloat16)
        weights[:, slot * plane:(slot + 1) * plane] = jnp.concatenate([upper, lower], axis=0)
    for kind in (0, 1):
        arrival(inner, kind)
        flatten(1 - odd, kind, field[inner, kind])
    for kind in (0, 1):
        arrival(last, kind)

    lowest = jnp.logical_and(space == 0, term < 2)
    highest = jnp.logical_and(space == spaces - 1, term >= total_terms - 2)
    for kind in (0, 1):
        values = [field[slot, kind] for slot in range(4)]
        values[0] = jnp.where(lowest, 0.0, values[0])
        values[3] = jnp.where(highest, 0.0, values[3])
        for slot in range(3):
            edges[kind, slot] = values[slot + 1] - values[slot]

    count = weights.shape[0] // 2

    def assemble(d):
        left = []
        for row in range(4):
            row = 4 * d + row
            borders = [edges[0, slot, pl.ds(row, 1), :] * edges[1, slot] for slot in range(3)]
            values = []
            for slot in (0, 1):
                value = borders[slot] + borders[slot + 1]
                for number in range(4 * slot, 4 * slot + 4):
                    value = value + flat[0, number, pl.ds(row, 1), :] * flat[1, number]
                values.append(value)
            value = jnp.concatenate(values, axis=1)
            upper = value.astype(jnp.bfloat16)
            left += [upper, (value - upper.astype(jnp.float32)).astype(jnp.bfloat16)]
        total = lax.dot_general(
            jnp.concatenate(left, axis=0), weights[...], (((1,), (1,)), ((), ())), preferred_element_type=jnp.float32,
        )
        total = total[:, :count] + total[:, count:]
        for row in range(4):
            at = 2 * row * modes
            part[d, row * modes:(row + 1) * modes, :] = total[at:at + modes] + total[at + modes:at + 2 * modes]

    def pair(n):
        return remote(
            part.at[place(n) * NC + 1 - c], pair_in.at[n], pair_sem.at[0, n], pair_sem.at[1, n],
            (place(places - 1) * NC + 1 - c, term),
        )

    def slab(n):
        return remote(mine.at[n], slab_in.at[n], slab_sem.at[0, n], slab_sem.at[1, n], (beside(n), term))

    def join(n):
        pair(n).wait_recv()
        mine[n] = part[place(n) * NC + c] + pair_in[n]

    def turn(n, carry):
        def step(k, carry):
            assemble(place(n) * NC + lax.rem(c + 1 + k, 2))
            return carry

        lax.fori_loop(0, 2, step, 0)
        pair(n).start()

        @pl.when(n > 0)
        def _():
            join(n - 1)

        @pl.when(jnp.logical_and(n > 4, n < 7))
        def _():
            slab(n - 5).wait_recv()
            mine[n - 1] = mine[n - 1] + slab_in[n - 5]

        @pl.when(jnp.logical_and(n > 0, n < 7))
        def _():
            slab(n - 1).start()

        return carry

    lax.fori_loop(0, places, turn, 0)
    for across in (1 - l, l):
        slab(3 - across).wait_recv()
        slab(4 + across).wait_recv()
    mine[6] = mine[6] + slab_in[2 + l] + slab_in[5 - l]
    near = remote(mine.at[6], near_in, near_sem.at[0], near_sem.at[1], (place(6) * NC + c, term))
    near.start()
    join(places - 1)
    total = mine[7] + slab_in[3 - l] + slab_in[4 + l]
    near.wait_recv()
    total = total + near_in[...]
    total = total.T
    turned[...] = total.reshape(turned.shape)
    sent = []
    for number, (step, other) in enumerate(owners):
        far_z, far_h = holder(step, other)
        sent.append(remote(
            turned.at[lax.div(far_h, 2), far_z], column_in.at[number], column_sem.at[0, number],
            column_sem.at[1, number], (space, far_z * NH + far_h),
        ))
        sent[-1].start()
    result = turned[lax.div(h, 2), z]
    for number, copy in enumerate(sent):
        copy.wait_recv()
        result = result + column_in[number]
    out_ref[...] = result

    for copy in first + relay + coeff + sent:
        copy.wait_send()
    for n in range(places):
        pair(n).wait_send()
    for n in range(6):
        slab(n).wait_send()
    near.wait_send()


def local(right_modes, adjoint_modes, conductivity_terms):
    modes, plane = right_modes.shape[1:]
    per = conductivity_terms.shape[1]
    spaces, places = NX * NL * NC, NX * NL
    block = (4 * modes, 2 * NZ * per)
    others = 2 * NZ - 1
    return pl.pallas_call(
        assemble_kernel,
        out_shape=jax.ShapeDtypeStruct((per, 4 * modes), jnp.float32),
        in_specs=[pl.BlockSpec(memory_space=pl.ANY)] * 3,
        out_specs=VMEM,
        scratch_shapes=[
            pltpu.VMEM((4, 2, modes, plane), jnp.float32),
            pltpu.VMEM((2, NZ, 2, per, plane), jnp.float32),
            pltpu.VMEM((2, 8, modes, plane), jnp.float32),
            pltpu.VMEM((2, 3, modes, plane), jnp.float32),
            pltpu.VMEM((4 * NZ * per, 2 * plane), jnp.bfloat16),
            pltpu.VMEM((spaces,) + block, jnp.float32),
            pltpu.VMEM((places,) + block, jnp.float32),
            pltpu.VMEM((places,) + block, jnp.float32),
            pltpu.VMEM((6,) + block, jnp.float32),
            pltpu.VMEM(block, jnp.float32),
            pltpu.VMEM((2, NZ, per, 4 * modes), jnp.float32),
            pltpu.VMEM((others, per, 4 * modes), jnp.float32),
            pltpu.SemaphoreType.DMA((3,)),
            pltpu.SemaphoreType.DMA((6,)),
            pltpu.SemaphoreType.DMA((4, 2)),
            pltpu.SemaphoreType.DMA((2, others)),
            pltpu.SemaphoreType.DMA((2, places)),
            pltpu.SemaphoreType.DMA((2, 6)),
            pltpu.SemaphoreType.DMA((2,)),
            pltpu.SemaphoreType.DMA((2, others)),
        ],
        compiler_params=pltpu.CompilerParams(collective_id=0, has_side_effects=True),
        name="assemble_blocks",
    )(right_modes, adjoint_modes, conductivity_terms)


def solution(mesh):
    placed = (
        P(("space", "term"), None, None),
        P(("space", "term"), None, None),
        P("space", "term", None),
    )
    return jax.shard_map(
        local, mesh=mesh, in_specs=placed, out_specs=P("term", "space"), check_vma=False
    )
```

```python
import jax
import jax.numpy as jnp
from jax import lax
from jax.experimental import pallas as pl
from jax.experimental.pallas import tpu as pltpu
from jax.sharding import PartitionSpec as P

MESH = pl.DeviceIdType.MESH
GY = 32
NX, NL, NC = 4, 2, 2
NZ, NH = 8, 4
VMEM = pl.BlockSpec(memory_space=pltpu.VMEM)


def moved(values, shift, keep):
    return jnp.where(keep, pltpu.roll(values, shift % values.shape[-1], values.ndim - 1), 0.0)


def assemble_kernel(
    right_ref, adjoint_ref, coeff_ref, out_ref,
    field, terms, flat, edges, inside, weights, part, pair_in, mine, slab_in, near_in, across_in, half_in, side_in,
    turned, column_in,
    own_sem, send_sem, recv_sem, term_sem, pair_sem, slab_sem, near_sem, across_sem, half_sem, side_sem, column_sem,
):
    spaces, total_terms, places = NX * NL * NC, NZ * NH, NX * NL
    modes, plane = field.shape[2:]
    space, term = lax.axis_index("space"), lax.axis_index("term")
    c = lax.rem(space, NC)
    x, l = lax.div(space, NL * NC), lax.rem(lax.div(space, NC), NL)
    z, h = lax.div(term, NH), lax.rem(term, NH)
    odd, mate = lax.rem(h, 2), NH - 1 - h
    index, planes = space * total_terms + term, spaces * total_terms

    def owner(number):
        return lax.div(number, total_terms), lax.rem(number, total_terms)

    above, below = owner(lax.rem(index + 1, planes)), owner(lax.rem(index + planes - 1, planes))
    partner_of_pair = owner(index + 1 - 2 * odd)
    owners = [(step, other) for step in range(NZ) for other in (0, 1)][1:]

    def holder(step, other):
        return lax.rem(z + step, NZ), (mate if other else h)

    def place(n):
        side = lax.rem(n, 2)
        away = jnp.where(n < 2, 2, jnp.where(n < 6, 1 + 2 * side, 0))
        here = jnp.where(n < 2, side, jnp.where(n < 4, 1 - side, side))
        return lax.rem(x + away, NX) * NL + lax.rem(l + 1 + here, NL)

    def beside(n):
        return (lax.rem(x + 1 + 2 * lax.rem(n, 2), NX) * NL + l) * NC + c

    def remote(src, dst, send, recv, target):
        return pltpu.make_async_remote_copy(
            src_ref=src, dst_ref=dst, send_sem=send, recv_sem=recv, device_id=target, device_id_type=MESH,
        )

    own = 1 + odd
    sources = (adjoint_ref.at[0], right_ref.at[0])
    brought = [pltpu.make_async_copy(sources[kind], field.at[own, kind], own_sem.at[kind]) for kind in (0, 1)]
    brought.append(pltpu.make_async_copy(
        coeff_ref.at[pl.ds(z * NH + 2 * lax.div(h, 2), 2)], terms.at[lax.div(h, 2), z], own_sem.at[2]
    ))
    for copy in brought:
        copy.start()

    barrier = pltpu.get_barrier_semaphore()
    partners = [above, below]
    for step, other in owners:
        far_z, far_h = holder(step, other)
        partners.append((space, far_z * NH + far_h))
    partners += [(beside(0), term), (beside(1), term), (place(6) * NC + c, term), (place(7) * NC + 1 - c, term)]
    for partner in partners:
        pl.semaphore_signal(barrier, inc=1, device_id=partner, device_id_type=MESH)
    pl.semaphore_wait(barrier, len(partners))

    def fresh(slot, kind, number, target):
        return remote(sources[kind], field.at[slot, kind], send_sem.at[number], recv_sem.at[slot, kind], target)

    def arrival(slot, kind):
        pltpu.make_async_copy(field.at[slot, kind], field.at[slot, kind], recv_sem.at[slot, kind]).wait()

    outward = tuple(jnp.where(odd == 1, up, down) for up, down in zip(above, below))
    to_outer = [fresh(3 - 3 * odd, kind, kind, outward) for kind in (0, 1)]
    to_inner = [fresh(own, kind, 2 + kind, partner_of_pair) for kind in (0, 1)]
    relay = [
        remote(
            field.at[3 * odd, kind], field.at[3 * odd, kind], send_sem.at[4 + kind], recv_sem.at[3 * odd, kind],
            partner_of_pair,
        )
        for kind in (0, 1)
    ]
    coeff = []
    for number, (step, other) in enumerate(owners):
        far_z, far_h = holder(step, other)
        coeff.append(remote(
            coeff_ref.at[pl.ds(far_z * NH + 2 * lax.div(far_h, 2), 2)], terms.at[lax.div(h, 2), z],
            term_sem.at[0, number], term_sem.at[1, number], (space, far_z * NH + far_h),
        ))
    to_outer[0].start()
    to_inner[0].start()
    for (step, other), copy in zip(owners, coeff):
        if not other:
            copy.start()

    cell = lax.broadcasted_iota(jnp.int32, (modes, plane), 1)
    in_row = lax.rem(cell, GY)
    keeps = ((GY, cell >= GY), (-GY, cell < plane - GY), (1, in_row != 0), (-1, in_row != GY - 1))

    def flatten(which, kind, values):
        for number, (shift, keep) in enumerate(keeps):
            flat[kind, 4 * which + number] = values - moved(values, shift, keep)

    def fill(which):
        def step(row, carry):
            value = None
            for number in range(4):
                product = flat[0, 4 * which + number, pl.ds(row, 1), :] * flat[1, 4 * which + number]
                value = product if value is None else value + product
            inside[which, row] = value
            return carry

        lax.fori_loop(0, modes, step, 0, unroll=4)

    for kind in (0, 1):
        brought[kind].wait()
        flatten(odd, kind, field[own, kind])
    fill(odd)

    outer, inner, last = 3 * odd, 2 - odd, 3 - 3 * odd
    for copies in (to_outer, to_inner):
        copies[0].wait_send()
        copies[1].start()
    arrival(outer, 0)
    relay[0].start()
    to_outer[1].wait_send()
    for (step, other), copy in zip(owners, coeff):
        if other:
            copy.start()
    arrival(outer, 1)
    relay[1].start()
    for kind in (0, 1):
        arrival(inner, kind)
        flatten(1 - odd, kind, field[inner, kind])
    fill(1 - odd)
    brought[2].wait()
    for copy in coeff:
        copy.wait_recv()
    for slot in (0, 1):
        value = 0.5 * terms[:, :, slot].reshape(-1, plane)
        upper = value.astype(jnp.bfloat16)
        lower = (value - upper.astype(jnp.float32)).astype(jnp.bfloat16)
        weights[:, slot * plane:(slot + 1) * plane] = jnp.concatenate([upper, lower], axis=0)
    for kind in (0, 1):
        arrival(last, kind)

    lowest = jnp.logical_and(space == 0, term < 2)
    highest = jnp.logical_and(space == spaces - 1, term >= total_terms - 2)
    for kind in (0, 1):
        values = [field[slot, kind] for slot in range(4)]
        values[0] = jnp.where(lowest, 0.0, values[0])
        values[3] = jnp.where(highest, 0.0, values[3])
        for slot in range(3):
            edges[kind, slot] = values[slot + 1] - values[slot]

    count = weights.shape[0] // 2

    def assemble(d):
        left = []
        for row in range(4):
            row = 4 * d + row
            borders = [edges[0, slot, pl.ds(row, 1), :] * edges[1, slot] for slot in range(3)]
            values = []
            for slot in (0, 1):
                values.append(borders[slot] + borders[slot + 1] + inside[slot, row])
            value = jnp.concatenate(values, axis=1)
            upper = value.astype(jnp.bfloat16)
            left += [upper, (value - upper.astype(jnp.float32)).astype(jnp.bfloat16)]
        total = lax.dot_general(
            jnp.concatenate(left, axis=0), weights[...], (((1,), (1,)), ((), ())), preferred_element_type=jnp.float32,
        )
        total = total[:, :count] + total[:, count:]
        for row in range(4):
            at = 2 * row * modes
            part[d, row * modes:(row + 1) * modes, :] = total[at:at + modes] + total[at + modes:at + 2 * modes]

    def pair(n):
        return remote(
            part.at[place(n) * NC + 1 - c], pair_in.at[n], pair_sem.at[0, n], pair_sem.at[1, n],
            (place(places - 1) * NC + 1 - c, term),
        )

    half = mine.shape[1] // 2
    quarter = half // 2
    first, second = pl.ds(0, half), pl.ds(half, half)
    beyond = (place(6) * NC + c, term)

    def slab(n):
        return remote(mine.at[n, first], slab_in.at[n], slab_sem.at[0, n], slab_sem.at[1, n], (beside(n), term))

    crossing = (0, 3, 4, 6)

    def cross(number):
        return remote(
            mine.at[crossing[number], second], across_in.at[number], across_sem.at[0, number],
            across_sem.at[1, number], beyond,
        )

    def part_way(side):
        return remote(
            mine.at[1, pl.ds(half + side * quarter, quarter)], half_in.at[side], half_sem.at[0, side],
            half_sem.at[1, side], (beside(side), term),
        )

    def sideways(side):
        return remote(
            mine.at[2 + 3 * side, second], side_in.at[side], side_sem.at[0, side], side_sem.at[1, side],
            (beside(side), term),
        )

    def join(n):
        pair(n).wait_recv()
        mine[n] = part[place(n) * NC + c] + pair_in[n]
        if n < 4:
            slab(n).start()
        if n in crossing:
            cross(crossing.index(n)).start()

    def turn(n, carry):
        def step(k, carry):
            assemble(place(n) * NC + lax.rem(c + 1 + k, 2))
            return carry

        lax.fori_loop(0, 2, step, 0)
        pair(n).start()
        for done in range(places - 1):
            @pl.when(n == done + 1)
            def _(done=done):
                join(done)

        return carry

    lax.fori_loop(0, places, turn, 0)
    for side in (0, 1):
        slab(side).wait_recv()
        mine[4 + side, first] = mine[4 + side, first] + slab_in[side]
        slab(4 + side).start()
    cross(0).wait_recv()
    mine[1, second] = mine[1, second] + across_in[0]
    for side in (0, 1):
        part_way(side).start()
    join(places - 1)
    for side in (1, 0):
        cross(2 - side).wait_recv()
        mine[2 + 3 * side, second] = mine[2 + 3 * side, second] + across_in[2 - side]
        part_way(side).wait_recv()
        rows = pl.ds(half + side * quarter, quarter)
        mine[2 + 3 * side, rows] = mine[2 + 3 * side, rows] + half_in[side]
        sideways(side).start()
    slab(3).wait_recv()
    slab(4).wait_recv()
    mine[6, first] = mine[6, first] + slab_in[3] + slab_in[4]
    near = remote(mine.at[6, first], near_in, near_sem.at[0], near_sem.at[1], beyond)
    near.start()
    slab(2).wait_recv()
    slab(5).wait_recv()
    upper = mine[7, first] + slab_in[2] + slab_in[5]
    cross(3).wait_recv()
    lower = mine[7, second] + across_in[3]
    for side in (0, 1):
        sideways(side).wait_recv()
        lower = lower + side_in[side]
    near.wait_recv()
    total = jnp.concatenate([upper + near_in[...], lower], axis=0)
    total = total.T
    turned[...] = total.reshape(turned.shape)
    sent = []
    for number, (step, other) in enumerate(owners):
        far_z, far_h = holder(step, other)
        sent.append(remote(
            turned.at[lax.div(far_h, 2), far_z], column_in.at[number], column_sem.at[0, number],
            column_sem.at[1, number], (space, far_z * NH + far_h),
        ))
        sent[-1].start()
    result = turned[lax.div(h, 2), z]
    for number, copy in enumerate(sent):
        copy.wait_recv()
        result = result + column_in[number]
    out_ref[...] = result

    for copy in to_inner[1:] + relay + coeff + sent:
        copy.wait_send()
    for n in range(places):
        pair(n).wait_send()
    for n in range(6):
        slab(n).wait_send()
    near.wait_send()
    for number in range(len(crossing)):
        cross(number).wait_send()
    for side in (0, 1):
        part_way(side).wait_send()
        sideways(side).wait_send()


def local(right_modes, adjoint_modes, conductivity_terms):
    modes, plane = right_modes.shape[1:]
    per = conductivity_terms.shape[1]
    spaces, places = NX * NL * NC, NX * NL
    block = (4 * modes, 2 * NZ * per)
    others = 2 * NZ - 1
    return pl.pallas_call(
        assemble_kernel,
        out_shape=jax.ShapeDtypeStruct((per, 4 * modes), jnp.float32),
        in_specs=[pl.BlockSpec(memory_space=pl.ANY)] * 3,
        out_specs=VMEM,
        scratch_shapes=[
            pltpu.VMEM((4, 2, modes, plane), jnp.float32),
            pltpu.VMEM((2, NZ, 2, per, plane), jnp.float32),
            pltpu.VMEM((2, 8, modes, plane), jnp.float32),
            pltpu.VMEM((2, 3, modes, plane), jnp.float32),
            pltpu.VMEM((2, modes, modes, plane), jnp.float32),
            pltpu.VMEM((4 * NZ * per, 2 * plane), jnp.bfloat16),
            pltpu.VMEM((spaces,) + block, jnp.float32),
            pltpu.VMEM((places,) + block, jnp.float32),
            pltpu.VMEM((places,) + block, jnp.float32),
            pltpu.VMEM((6, 2 * modes, block[1]), jnp.float32),
            pltpu.VMEM((2 * modes, block[1]), jnp.float32),
            pltpu.VMEM((4, 2 * modes, block[1]), jnp.float32),
            pltpu.VMEM((2, modes, block[1]), jnp.float32),
            pltpu.VMEM((2, 2 * modes, block[1]), jnp.float32),
            pltpu.VMEM((2, NZ, per, 4 * modes), jnp.float32),
            pltpu.VMEM((others, per, 4 * modes), jnp.float32),
            pltpu.SemaphoreType.DMA((3,)),
            pltpu.SemaphoreType.DMA((6,)),
            pltpu.SemaphoreType.DMA((4, 2)),
            pltpu.SemaphoreType.DMA((2, others)),
            pltpu.SemaphoreType.DMA((2, places)),
            pltpu.SemaphoreType.DMA((2, 6)),
            pltpu.SemaphoreType.DMA((2,)),
            pltpu.SemaphoreType.DMA((2, 4)),
            pltpu.SemaphoreType.DMA((2, 2)),
            pltpu.SemaphoreType.DMA((2, 2)),
            pltpu.SemaphoreType.DMA((2, others)),
        ],
        compiler_params=pltpu.CompilerParams(collective_id=0, has_side_effects=True),
        name="assemble_blocks",
    )(right_modes, adjoint_modes, conductivity_terms)


def solution(mesh):
    placed = (
        P(("space", "term"), None, None),
        P(("space", "term"), None, None),
        P("space", "term", None),
    )
    return jax.shard_map(
        local, mesh=mesh, in_specs=placed, out_specs=P("term", "space"), check_vma=False
    )
```

```python
import jax
import jax.numpy as jnp
from jax import lax
from jax.experimental import pallas as pl
from jax.experimental.pallas import tpu as pltpu
from jax.sharding import PartitionSpec as P

MESH = pl.DeviceIdType.MESH
GY = 32
NX, NL, NC = 4, 2, 2
NZ, NH = 8, 4
VMEM = pl.BlockSpec(memory_space=pltpu.VMEM)


def moved(values, shift, keep):
    return jnp.where(keep, pltpu.roll(values, shift % values.shape[-1], values.ndim - 1), 0.0)


def assemble_kernel(
    right_ref, adjoint_ref, coeff_ref, out_ref,
    field, terms, flat, edges, inside, weights, part, pair_in, mine, slab_in, near_in, across_in, half_in, side_in,
    turned, column_in,
    own_sem, send_sem, recv_sem, term_sem, pair_sem, slab_sem, near_sem, across_sem, half_sem, side_sem, column_sem,
):
    spaces, total_terms, places = NX * NL * NC, NZ * NH, NX * NL
    modes, plane = field.shape[2:]
    space, term = lax.axis_index("space"), lax.axis_index("term")
    c = lax.rem(space, NC)
    x, l = lax.div(space, NL * NC), lax.rem(lax.div(space, NC), NL)
    z, h = lax.div(term, NH), lax.rem(term, NH)
    odd, mate = lax.rem(h, 2), NH - 1 - h
    index, planes = space * total_terms + term, spaces * total_terms

    def owner(number):
        return lax.div(number, total_terms), lax.rem(number, total_terms)

    above, below = owner(lax.rem(index + 1, planes)), owner(lax.rem(index + planes - 1, planes))
    partner_of_pair = owner(index + 1 - 2 * odd)
    steps = sorted(range(NZ), key=lambda step: abs(2 * step - NZ))
    owners = [(step, other) for step in steps for other in (0, 1) if step or other]

    def holder(step, other):
        return lax.rem(z + step, NZ), (mate if other else h)

    def place(n):
        side = lax.rem(n, 2)
        away = jnp.where(n < 2, 2, jnp.where(n < 6, 1 + 2 * side, 0))
        here = jnp.where(n < 2, side, jnp.where(n < 4, 1 - side, side))
        return lax.rem(x + away, NX) * NL + lax.rem(l + 1 + here, NL)

    def beside(n):
        return (lax.rem(x + 1 + 2 * lax.rem(n, 2), NX) * NL + l) * NC + c

    def remote(src, dst, send, recv, target):
        return pltpu.make_async_remote_copy(
            src_ref=src, dst_ref=dst, send_sem=send, recv_sem=recv, device_id=target, device_id_type=MESH,
        )

    own = 1 + odd
    sources = (adjoint_ref.at[0], right_ref.at[0])
    brought = [pltpu.make_async_copy(sources[kind], field.at[own, kind], own_sem.at[kind]) for kind in (0, 1)]
    brought.append(pltpu.make_async_copy(
        coeff_ref.at[pl.ds(z * NH + 2 * lax.div(h, 2), 2)], terms.at[lax.div(h, 2), z], own_sem.at[2]
    ))
    for copy in brought:
        copy.start()

    barrier = pltpu.get_barrier_semaphore()
    partners = [above, below]
    for step, other in owners:
        far_z, far_h = holder(step, other)
        partners.append((space, far_z * NH + far_h))
    partners += [(beside(0), term), (beside(1), term), (place(6) * NC + c, term), (place(7) * NC + 1 - c, term)]
    for partner in partners:
        pl.semaphore_signal(barrier, inc=1, device_id=partner, device_id_type=MESH)
    pl.semaphore_wait(barrier, len(partners))

    def fresh(slot, kind, number, target):
        return remote(sources[kind], field.at[slot, kind], send_sem.at[number], recv_sem.at[slot, kind], target)

    def arrival(slot, kind):
        pltpu.make_async_copy(field.at[slot, kind], field.at[slot, kind], recv_sem.at[slot, kind]).wait()

    outward = tuple(jnp.where(odd == 1, up, down) for up, down in zip(above, below))
    to_outer = [fresh(3 - 3 * odd, kind, kind, outward) for kind in (0, 1)]
    to_inner = [fresh(own, kind, 2 + kind, partner_of_pair) for kind in (0, 1)]
    relay = [
        remote(
            field.at[3 * odd, kind], field.at[3 * odd, kind], send_sem.at[4 + kind], recv_sem.at[3 * odd, kind],
            partner_of_pair,
        )
        for kind in (0, 1)
    ]
    coeff = []
    for number, (step, other) in enumerate(owners):
        far_z, far_h = holder(step, other)
        coeff.append(remote(
            coeff_ref.at[pl.ds(far_z * NH + 2 * lax.div(far_h, 2), 2)], terms.at[lax.div(h, 2), z],
            term_sem.at[0, number], term_sem.at[1, number], (space, far_z * NH + far_h),
        ))
    for copy in to_outer + to_inner:
        copy.start()
    for crossed in (0, 1):
        for (step, other), copy in zip(owners, coeff):
            if other == crossed:
                copy.start()

    cell = lax.broadcasted_iota(jnp.int32, (modes, plane), 1)
    in_row = lax.rem(cell, GY)
    keeps = ((GY, cell >= GY), (-GY, cell < plane - GY), (1, in_row != 0), (-1, in_row != GY - 1))

    def flatten(which, kind, values):
        for number, (shift, keep) in enumerate(keeps):
            flat[kind, 4 * which + number] = values - moved(values, shift, keep)

    def fill(which):
        def step(row, carry):
            value = None
            for number in range(4):
                product = flat[0, 4 * which + number, pl.ds(row, 1), :] * flat[1, 4 * which + number]
                value = product if value is None else value + product
            inside[which, row] = value
            return carry

        lax.fori_loop(0, modes, step, 0, unroll=4)

    for kind in (0, 1):
        brought[kind].wait()
        flatten(odd, kind, field[own, kind])
    fill(odd)

    outer, inner, last = 3 * odd, 2 - odd, 3 - 3 * odd
    for kind in (0, 1):
        arrival(outer, kind)
        relay[kind].start()
    for kind in (0, 1):
        arrival(inner, kind)
        flatten(1 - odd, kind, field[inner, kind])
    fill(1 - odd)
    brought[2].wait()
    for copy in coeff:
        copy.wait_recv()
    for slot in (0, 1):
        value = 0.5 * terms[:, :, slot].reshape(-1, plane)
        upper = value.astype(jnp.bfloat16)
        lower = (value - upper.astype(jnp.float32)).astype(jnp.bfloat16)
        weights[:, slot * plane:(slot + 1) * plane] = jnp.concatenate([upper, lower], axis=0)
    for kind in (0, 1):
        arrival(last, kind)

    lowest = jnp.logical_and(space == 0, term < 2)
    highest = jnp.logical_and(space == spaces - 1, term >= total_terms - 2)
    for kind in (0, 1):
        values = [field[slot, kind] for slot in range(4)]
        values[0] = jnp.where(lowest, 0.0, values[0])
        values[3] = jnp.where(highest, 0.0, values[3])
        for slot in range(3):
            edges[kind, slot] = values[slot + 1] - values[slot]

    count = weights.shape[0] // 2

    def assemble(blocks):
        left = []
        for row in [4 * d + row for d in blocks for row in range(4)]:
            borders = [edges[0, slot, pl.ds(row, 1), :] * edges[1, slot] for slot in range(3)]
            values = []
            for slot in (0, 1):
                values.append(borders[slot] + borders[slot + 1] + inside[slot, row])
            value = jnp.concatenate(values, axis=1)
            upper = value.astype(jnp.bfloat16)
            left += [upper, (value - upper.astype(jnp.float32)).astype(jnp.bfloat16)]
        total = lax.dot_general(
            jnp.concatenate(left, axis=0), weights[...], (((1,), (1,)), ((), ())), preferred_element_type=jnp.float32,
        )
        total = total[:, :count] + total[:, count:]
        for number, d in enumerate(blocks):
            for row in range(4):
                at = 2 * (4 * number + row) * modes
                part[d, row * modes:(row + 1) * modes, :] = total[at:at + modes] + total[at + modes:at + 2 * modes]

    def pair(n):
        return remote(
            part.at[place(n) * NC + 1 - c], pair_in.at[n], pair_sem.at[0, n], pair_sem.at[1, n],
            (place(places - 1) * NC + 1 - c, term),
        )

    half = mine.shape[1] // 2
    quarter = half // 2
    first, second = pl.ds(0, half), pl.ds(half, half)
    beyond = (place(6) * NC + c, term)

    def slab(n):
        return remote(mine.at[n, first], slab_in.at[n], slab_sem.at[0, n], slab_sem.at[1, n], (beside(n), term))

    crossing = (0, 3, 4, 6)

    def cross(number):
        return remote(
            mine.at[crossing[number], second], across_in.at[number], across_sem.at[0, number],
            across_sem.at[1, number], beyond,
        )

    def part_way(side):
        return remote(
            mine.at[1, pl.ds(half + side * quarter, quarter)], half_in.at[side], half_sem.at[0, side],
            half_sem.at[1, side], (beside(side), term),
        )

    def sideways(side):
        return remote(
            mine.at[2 + 3 * side, second], side_in.at[side], side_sem.at[0, side], side_sem.at[1, side],
            (beside(side), term),
        )

    def join(n):
        pair(n).wait_recv()
        mine[n] = part[place(n) * NC + c] + pair_in[n]
        if n < 4:
            slab(n).start()
        if n in crossing:
            cross(crossing.index(n)).start()

    def turn(n, carry):
        assemble([place(n) * NC + 1 - c, place(n) * NC + c])
        pair(n).start()
        for done in range(places - 1):
            @pl.when(n == done + 1)
            def _(done=done):
                join(done)
                if done in (4, 5):
                    side = done - 4
                    slab(side).wait_recv()
                    mine[done, first] = mine[done, first] + slab_in[side]
                    slab(done).start()
                if done == 5:
                    cross(0).wait_recv()
                    mine[1, second] = mine[1, second] + across_in[0]
                    for side in (0, 1):
                        part_way(side).start()

        return carry

    lax.fori_loop(0, places, turn, 0)
    join(places - 1)
    for side in (1, 0):
        cross(2 - side).wait_recv()
        mine[2 + 3 * side, second] = mine[2 + 3 * side, second] + across_in[2 - side]
        part_way(side).wait_recv()
        rows = pl.ds(half + side * quarter, quarter)
        mine[2 + 3 * side, rows] = mine[2 + 3 * side, rows] + half_in[side]
        sideways(side).start()
    slab(3).wait_recv()
    slab(4).wait_recv()
    mine[6, first] = mine[6, first] + slab_in[3] + slab_in[4]
    near = remote(mine.at[6, first], near_in, near_sem.at[0], near_sem.at[1], beyond)
    near.start()
    slab(2).wait_recv()
    slab(5).wait_recv()
    upper = mine[7, first] + slab_in[2] + slab_in[5]
    cross(3).wait_recv()
    lower = mine[7, second] + across_in[3]
    for side in (0, 1):
        sideways(side).wait_recv()
        lower = lower + side_in[side]
    near.wait_recv()
    total = jnp.concatenate([upper + near_in[...], lower], axis=0)
    total = total.T
    turned[...] = total.reshape(turned.shape)
    sent = []
    for number, (step, other) in enumerate(owners):
        far_z, far_h = holder(step, other)
        sent.append(remote(
            turned.at[lax.div(far_h, 2), far_z], column_in.at[number], column_sem.at[0, number],
            column_sem.at[1, number], (space, far_z * NH + far_h),
        ))
        sent[-1].start()
    result = turned[lax.div(h, 2), z]
    for number, copy in enumerate(sent):
        copy.wait_recv()
        result = result + column_in[number]
    out_ref[...] = result

    for copy in to_outer + to_inner + relay + coeff + sent:
        copy.wait_send()
    for n in range(places):
        pair(n).wait_send()
    for n in range(6):
        slab(n).wait_send()
    near.wait_send()
    for number in range(len(crossing)):
        cross(number).wait_send()
    for side in (0, 1):
        part_way(side).wait_send()
        sideways(side).wait_send()


def local(right_modes, adjoint_modes, conductivity_terms):
    modes, plane = right_modes.shape[1:]
    per = conductivity_terms.shape[1]
    spaces, places = NX * NL * NC, NX * NL
    block = (4 * modes, 2 * NZ * per)
    others = 2 * NZ - 1
    return pl.pallas_call(
        assemble_kernel,
        out_shape=jax.ShapeDtypeStruct((per, 4 * modes), jnp.float32),
        in_specs=[pl.BlockSpec(memory_space=pl.ANY)] * 3,
        out_specs=VMEM,
        scratch_shapes=[
            pltpu.VMEM((4, 2, modes, plane), jnp.float32),
            pltpu.VMEM((2, NZ, 2, per, plane), jnp.float32),
            pltpu.VMEM((2, 8, modes, plane), jnp.float32),
            pltpu.VMEM((2, 3, modes, plane), jnp.float32),
            pltpu.VMEM((2, modes, modes, plane), jnp.float32),
            pltpu.VMEM((4 * NZ * per, 2 * plane), jnp.bfloat16),
            pltpu.VMEM((spaces,) + block, jnp.float32),
            pltpu.VMEM((places,) + block, jnp.float32),
            pltpu.VMEM((places,) + block, jnp.float32),
            pltpu.VMEM((6, 2 * modes, block[1]), jnp.float32),
            pltpu.VMEM((2 * modes, block[1]), jnp.float32),
            pltpu.VMEM((4, 2 * modes, block[1]), jnp.float32),
            pltpu.VMEM((2, modes, block[1]), jnp.float32),
            pltpu.VMEM((2, 2 * modes, block[1]), jnp.float32),
            pltpu.VMEM((2, NZ, per, 4 * modes), jnp.float32),
            pltpu.VMEM((others, per, 4 * modes), jnp.float32),
            pltpu.SemaphoreType.DMA((3,)),
            pltpu.SemaphoreType.DMA((6,)),
            pltpu.SemaphoreType.DMA((4, 2)),
            pltpu.SemaphoreType.DMA((2, others)),
            pltpu.SemaphoreType.DMA((2, places)),
            pltpu.SemaphoreType.DMA((2, 6)),
            pltpu.SemaphoreType.DMA((2,)),
            pltpu.SemaphoreType.DMA((2, 4)),
            pltpu.SemaphoreType.DMA((2, 2)),
            pltpu.SemaphoreType.DMA((2, 2)),
            pltpu.SemaphoreType.DMA((2, others)),
        ],
        compiler_params=pltpu.CompilerParams(collective_id=0, has_side_effects=True),
        name="assemble_blocks",
    )(right_modes, adjoint_modes, conductivity_terms)


def solution(mesh):
    placed = (
        P(("space", "term"), None, None),
        P(("space", "term"), None, None),
        P("space", "term", None),
    )
    return jax.shard_map(
        local, mesh=mesh, in_specs=placed, out_specs=P("term", "space"), check_vma=False
    )
```
